32 devices in a mesh: rows: 8 (over z, x), samp: 4 (over y, core).
Axes of the slice: x: 2, y: 2, z: 4, core: 2. Of those that a mesh axis runs over, the one named last changes fastest.
Arguments:
- noise: bfloat16 [6, 64, 512, 128], P(None, 'rows', 'samp'), may hold values from -6 to 6
- diag_inverse: bfloat16 [6, 64, 128, 128], P(None, 'rows'), may hold values from -0.5 to 0.5
- coupling: bfloat16 [5, 64, 16, 128, 128], P(None, 'rows'), may hold values from -0.125 to 0.125
- pattern: int32 [5, 64, 16], P(None, 'rows'), may hold values from 0 to 319, as said below
Outputs:
- samples: bfloat16 [6, 64, 512, 128], P(None, 'rows', 'samp')
- variance: float32 [6, 64, 128], P(None, 'rows')
The draws below stay inside these ranges and needn't reach their ends.
Inputs may be any that keep to these rules, and one draw needn't show every extreme that they name: pattern[l, s, k] names a block row of a level before l + 1; the entry k = 0 lies in level l; entries may repeat. Block rows s with equal s // 8 together name, within any one level, at most one of the block rows t that share one value of t // 8.
All inputs are finite; a program needn't handle non-finite values.
Results may differ from the reference program's by a relative error of at most 0.008.
Values may be sent and summed in bfloat16 or wider, within the bound.
A program may use at most 192 MiB of HBM per device.

```python
import jax
import jax.numpy as jnp

B = 128
LEVELS = 6
K = 16
SLOT_DEV = 8
SLOTS = 64
S = 512


def draw_pattern(key, part):
    table_key, level_key, device_key = jax.random.split(key, 3)
    device_count = SLOTS // SLOT_DEV
    table = jax.random.randint(table_key, (device_count, LEVELS - 1, device_count), 0, SLOT_DEV)
    level_ids = jnp.arange(LEVELS - 1, dtype=jnp.int32)[:, None, None]
    drawn = jax.random.randint(level_key, (LEVELS - 1, SLOTS, K), 0, level_ids + 1)
    first = jnp.broadcast_to(level_ids, (LEVELS - 1, SLOTS, 1))
    source = jnp.concatenate([first, drawn[:, :, 1:]], axis=2).astype(jnp.int32)
    device_ids = jax.random.randint(device_key, (LEVELS - 1, SLOTS, K), 0, device_count)
    owner = (jnp.arange(SLOTS, dtype=jnp.int32) // SLOT_DEV)[None, :, None]
    flat = (owner * (LEVELS - 1) + source) * device_count + device_ids
    chosen = jnp.take(table.reshape(-1), flat)
    return (source * SLOTS + device_ids * SLOT_DEV + chosen).astype(jnp.int32)


def levels(rng, shape, pieces, low, largest):
    def one(dim, shards_of):
        steps = jax.random.uniform(jax.random.fold_in(jax.random.fold_in(rng, 6), dim), (shards_of,), jnp.float32, low / len(pieces), largest / len(pieces))
        return jnp.repeat(jnp.exp(steps), shape[dim] // shards_of).reshape((-1,) + (1,) * (len(shape) - dim - 1))

    level = one(*pieces[0])
    for cut in pieces[1:]:
        level = level * one(*cut)
    return level


def centred(key, shape, scale, limit, pieces=(), kind=jnp.bfloat16):
    result = jax.random.normal(key, shape, jnp.float32) * scale
    if len(pieces) > 0:
        result = levels(key, shape, pieces, -0.22, 0.18) * result
    return jnp.clip(result, min=-limit, max=limit).astype(kind)


def setup_inputs(seed: int = 0) -> dict:
    arg_keys = jax.random.split(jax.random.key(seed), 5)
    return {
        "noise": centred(arg_keys[0], (LEVELS, SLOTS, S, B), 1.0, 6.0, ((1, 8), (2, 4))),
        "diag_inverse": centred(arg_keys[1], (LEVELS, SLOTS, B, B), B ** -0.5, 0.5, ((1, 8),)),
        "coupling": centred(arg_keys[2], (LEVELS - 1, SLOTS, K, B, B), (B * K) ** -0.5, 0.125, ((1, 8),)),
        "pattern": draw_pattern(jax.random.fold_in(arg_keys[4], 71), 0),
    }


def reference(noise, diag_inverse, coupling, pattern):
    solved = []
    for level_index in range(LEVELS):
        if level_index == 0:
            residual = noise[0].astype(jnp.float32)
        else:
            solved_rows = jnp.concatenate(solved, axis=0)
            picked = jnp.take(solved_rows, pattern[level_index - 1].astype(jnp.int32), axis=0)
            update = jnp.einsum("pksb,pkbc->psc", picked.astype(jnp.float32), coupling[level_index - 1].astype(jnp.float32))
            residual = noise[level_index].astype(jnp.float32) - update
        rounded = residual.astype(jnp.bfloat16)
        block = jnp.einsum("psb,pbc->psc", rounded.astype(jnp.float32), diag_inverse[level_index].astype(jnp.float32))
        solved.append(block.astype(jnp.bfloat16))
    samples = jnp.stack(solved, axis=0)
    wide = samples.astype(jnp.float32)
    variance = jnp.mean(wide * wide, axis=2)
    return samples, variance
```

```python
import functools

import jax
import jax.numpy as jnp
from jax import lax
from jax.experimental import pallas as pl
from jax.experimental.pallas import tpu as pltpu
from jax.sharding import PartitionSpec as P

MESH = pl.DeviceIdType.MESH
F32 = jnp.float32
BF16 = jnp.bfloat16
I32 = jnp.int32

CHUNKS = 2
GROUP = 2


def kernel(
    n, m, pat_hbm, noise_hbm, diag_hbm, coup_hbm,
    samples_hbm, var_ref,
    pat, patv, noise, diag, own, placed, table, send, recv,
    need, want_s, want_v, index_v, index, sums, vrecv,
    pat_sem, noise_sem, diag_sem, coup_sem, out_sem, send_sem, recv_sem,
    nsend_sem, nrecv_sem, index_sem, vsend_sem, vrecv_sem, *coup,
):
    levels, slot_dev, samp, b = noise.shape
    fan = pat.shape[2]
    me = lax.axis_index("rows")
    q = lax.axis_index("samp")
    part = samp // CHUNKS
    order = list(range(n - 1, 0, -1))

    def partner(p):
        other, bit = me, 1
        while bit < n:
            if p & bit:
                other = other + bit - 2 * bit * lax.rem(lax.div(me, bit), 2)
            bit *= 2
        return other

    barrier = pltpu.get_barrier_semaphore()
    for p in order:
        pl.semaphore_signal(
            barrier, inc=1, device_id={"rows": partner(p)}, device_id_type=MESH
        )
    for o in range(1, m):
        pl.semaphore_signal(
            barrier, inc=1, device_id={"samp": lax.rem(q + o, m)}, device_id_type=MESH
        )

    def fetch(src, dst, sem, i):
        return pltpu.make_async_copy(src.at[i], dst.at[i], sem.at[i])

    def coup_fetch(i):
        return pltpu.make_async_copy(coup_hbm.at[i], coup[i], coup_sem.at[i])

    pat_v_copy = pltpu.make_async_copy(pat_hbm, patv, pat_sem.at[0])
    pat_s_copy = pltpu.make_async_copy(pat_hbm, pat, pat_sem.at[1])
    pat_v_copy.start()
    pat_s_copy.start()
    fetch(noise_hbm, noise, noise_sem, 0).start()
    fetch(diag_hbm, diag, diag_sem, 0).start()

    pat_v_copy.wait()
    shape = (n, 8, fan)
    dev = lax.broadcasted_iota(I32, shape, 0)
    lev = lax.broadcasted_iota(I32, shape, 1)
    key = lev * n + dev
    best = jnp.zeros(shape, I32)
    for t in range(levels - 1):
        for s in range(slot_dev):
            entry = patv[t, s : s + 1, :].reshape(1, 1, fan)
            holder = lax.div(entry, jnp.int32(slot_dev))
            slot = entry - holder * slot_dev
            best = jnp.maximum(best, jnp.where(holder == key, slot, 0))
    best = jnp.broadcast_to(jnp.max(best, axis=2, keepdims=True), (n, 8, 128))
    row = lax.broadcasted_iota(I32, (n, 8, 128), 1)
    lane = lax.broadcasted_iota(I32, (n, 8, 128), 2)
    need[...] = jnp.sum(jnp.where(row == lane, best, 0), axis=1, keepdims=True)

    def need_copy(p):
        return pltpu.make_async_remote_copy(
            src_ref=need.at[partner(p)],
            dst_ref=want_v.at[p - 1],
            send_sem=nsend_sem.at[p - 1],
            recv_sem=nrecv_sem.at[p - 1],
            device_id={"rows": partner(p)},
            device_id_type=MESH,
        )

    def block_copy(level, h, p):
        return pltpu.make_async_remote_copy(
            src_ref=send.at[level, h, p - 1],
            dst_ref=recv.at[level, h, p - 1],
            send_sem=send_sem.at[level, h],
            recv_sem=recv_sem.at[level, h],
            device_id={"rows": partner(p)},
            device_id_type=MESH,
        )

    def chunk_copy(level, h):
        return pltpu.make_async_remote_copy(
            src_ref=send.at[level, h],
            dst_ref=recv.at[level, h],
            send_sem=send_sem.at[level, h],
            recv_sem=recv_sem.at[level, h],
            device_id={"rows": partner(1)},
            device_id_type=MESH,
        )

    def solve(level, s, h):
        residual = noise[level, s, pl.ds(h * part, part), :].astype(F32)
        total = None
        for k in range(0, fan, 2):
            picked = [
                table[h, lax.div(pat[level - 1, s, k + j], jnp.int32(slot_dev))]
                for j in range(2)
            ]
            term = jnp.dot(
                jnp.concatenate(picked, axis=1),
                coup[level - 1][s, pl.ds(k * b, 2 * b), :],
                preferred_element_type=F32,
            )
            total = term if total is None else total + term
        return jnp.dot(
            (residual - total).astype(BF16), diag[level, s], preferred_element_type=F32
        ).astype(BF16)

    def squares(x):
        wide = x.astype(F32)
        return jnp.sum(wide * wide, axis=0, keepdims=True)

    def receive(level, h):
        chunk_copy(level, h).wait_recv()
        for p in order:
            table[h, level * n + partner(p)] = recv[level, h, p - 1]

    def write_out(level):
        return pltpu.make_async_copy(own.at[level], samples_hbm.at[level], out_sem.at[level])

    pl.semaphore_wait(barrier, n - 1 + m - 1)
    for p in order:
        need_copy(p).start()
    for i in range(1, levels):
        fetch(noise_hbm, noise, noise_sem, i).start()
        fetch(diag_hbm, diag, diag_sem, i).start()
    coup_fetch(0).start()

    fetch(noise_hbm, noise, noise_sem, 0).wait()
    fetch(diag_hbm, diag, diag_sem, 0).wait()
    for s in range(slot_dev):
        x = jnp.dot(noise[0, s], diag[0, s], preferred_element_type=F32).astype(BF16)
        own[0, s] = x
        sums[0, pl.ds(s, 1), :] = squares(x)

    for p in order:
        need_copy(p).wait_recv()
    copy = pltpu.make_async_copy(want_v, want_s, index_sem)
    copy.start()
    copy.wait()
    for h in range(CHUNKS):
        for p in order:
            send[0, h, p - 1] = own[0, want_s[p - 1, 0, 0], pl.ds(h * part, part), :]
            block_copy(0, h, p).start()
    coup_fetch(1).start()
    write_out(0).start()

    mine = need[me]
    wants = [want_v[p - 1] for p in order] + [mine]
    slots = lax.broadcasted_iota(I32, (slot_dev, 128), 0)
    first = slots + n
    for i in range(n - 2, -1, -1):
        first = jnp.where(wants[i] == slots, i, first)
    rank = jnp.zeros((slot_dev, 128), I32)
    for s in range(slot_dev):
        rank = rank + (first[s : s + 1] < first).astype(I32)
    turn = jnp.zeros((slot_dev, 128), I32)
    for s in range(slot_dev):
        turn = turn + jnp.where(rank[s : s + 1] == slots, s, 0)
    index_v[pl.ds(0, slot_dev), :] = turn
    index_v[pl.ds(slot_dev, slot_dev), :] = rank
    for i in range(n):
        index_v[pl.ds(2 * slot_dev + i, 1), :] = jnp.sum(
            jnp.where(wants[i] == slots, rank, 0), axis=0, keepdims=True
        )
    index_v[pl.ds(2 * slot_dev + n, 1), :] = mine
    copy = pltpu.make_async_copy(index_v, index, index_sem)
    copy.start()
    copy.wait()
    pat_s_copy.wait()

    for h in range(CHUNKS):
        table[h, me] = own[0, index[2 * slot_dev + n, 0], pl.ds(h * part, part), :]
    for level in range(1, levels):
        fetch(noise_hbm, noise, noise_sem, level).wait()
        fetch(diag_hbm, diag, diag_sem, level).wait()

    for level in range(1, levels - 1):
        coup_fetch(level - 1).wait()
        for h in range(CHUNKS):
            rows = pl.ds(h * part, part)
            receive(level - 1, h)
            for low in range(0, slot_dev, GROUP):
                high = min(low + GROUP, slot_dev)
                for i in range(low, high):
                    placed[level - 1, i, rows, :] = solve(level, index[i, level], h)
                dests = range(low, min(high, n - 1) if high < slot_dev else n - 1)
                for i in dests:
                    at = index[2 * slot_dev + i, level]
                    send[level, h, order[i] - 1] = placed[level - 1, at, rows, :]
                for i in dests:
                    block_copy(level, h, order[i]).start()
            if h == CHUNKS - 1 and level + 1 < levels - 1:
                coup_fetch(level + 1).start()
            table[h, level * n + me] = placed[
                level - 1, index[2 * slot_dev + n - 1, level], rows, :
            ]
        for s in range(slot_dev):
            x = placed[level - 1, index[slot_dev + s, level]]
            own[level, s] = x
            sums[level, pl.ds(s, 1), :] = squares(x)
        write_out(level).start()

    last = levels - 1

    def var_copy(o, i):
        at = (pl.ds(0, last), pl.ds(last, 1))[i]
        return pltpu.make_async_remote_copy(
            src_ref=sums.at[at],
            dst_ref=vrecv.at[o - 1, at],
            send_sem=vsend_sem.at[i, o - 1],
            recv_sem=vrecv_sem.at[i, o - 1],
            device_id={"samp": lax.rem(q + o, m)},
            device_id_type=MESH,
        )

    for o in range(1, m):
        var_copy(o, 0).start()
    coup_fetch(last - 1).wait()
    for h in range(CHUNKS):
        rows = pl.ds(h * part, part)
        receive(last - 1, h)
        for s in range(slot_dev):
            x = solve(last, s, h)
            own[last, s, rows, :] = x
            found = squares(x)
            if h > 0:
                found = found + sums[last, pl.ds(s, 1), :]
            sums[last, pl.ds(s, 1), :] = found
    for o in range(1, m):
        var_copy(o, 1).start()
    write_out(last).start()
    for level in range(levels - 1):
        write_out(level).wait()
        for h in range(CHUNKS):
            chunk_copy(level, h).wait_send()
    for p in order:
        need_copy(p).wait_send()
    for i in range(2):
        for o in range(1, m):
            var_copy(o, i).wait()
    total = sums[...]
    for o in range(1, m):
        total = total + vrecv[o - 1]
    var_ref[...] = total * (1.0 / (samp * m))
    write_out(last).wait()


def hand_out(x_hbm, v_hbm, y_hbm, w_hbm, x, v, in_sem, out_sem, v_sem):
    levels = x.shape[0]
    reads = [pltpu.make_async_copy(x_hbm.at[i], x.at[i], in_sem.at[i]) for i in range(levels)]
    writes = [pltpu.make_async_copy(x.at[i], y_hbm.at[i], out_sem.at[i]) for i in range(levels)]
    v_read = pltpu.make_async_copy(v_hbm, v, v_sem.at[0])
    v_write = pltpu.make_async_copy(v, w_hbm, v_sem.at[1])
    v_read.start()
    for copy in reads:
        copy.start()
    v_read.wait()
    v_write.start()
    for i in range(levels):
        reads[i].wait()
        writes[i].start()
    v_write.wait()
    for copy in writes:
        copy.wait()


def body(n, m, noise, diag, coupling, pattern):
    levels, slot_dev, samp, b = noise.shape
    fan = coupling.shape[2]
    part = samp // CHUNKS
    any_spec = pl.BlockSpec(memory_space=pl.ANY)
    vmem_spec = pl.BlockSpec(memory_space=pltpu.VMEM)
    dma = pltpu.SemaphoreType.DMA
    coupling = coupling.reshape(levels - 1, slot_dev, fan * b, b)
    lines = 2 * slot_dev + -(-(n + 1) // 8) * 8
    solved = pl.pallas_call(
        functools.partial(kernel, n, m),
        out_shape=(
            jax.ShapeDtypeStruct(noise.shape, BF16),
            jax.ShapeDtypeStruct((levels, slot_dev, b), F32),
        ),
        in_specs=[any_spec] * 4,
        out_specs=(any_spec, vmem_spec),
        scratch_shapes=[
            pltpu.SMEM(pattern.shape, I32),
            pltpu.VMEM(pattern.shape, I32),
            pltpu.VMEM(noise.shape, BF16),
            pltpu.VMEM(diag.shape, BF16),
            pltpu.VMEM(noise.shape, BF16),
            pltpu.VMEM((levels - 2, slot_dev, samp, b), BF16),
            pltpu.VMEM((CHUNKS, (levels - 1) * n, part, b), BF16),
            pltpu.VMEM((levels - 1, CHUNKS, n - 1, part, b), BF16),
            pltpu.VMEM((levels - 1, CHUNKS, n - 1, part, b), BF16),
            pltpu.VMEM((n, 1, 128), I32),
            pltpu.SMEM((n - 1, 1, 128), I32),
            pltpu.VMEM((n - 1, 1, 128), I32),
            pltpu.VMEM((lines, 128), I32),
            pltpu.SMEM((lines, 128), I32),
            pltpu.VMEM((levels, slot_dev, b), F32),
            pltpu.VMEM((m - 1, levels, slot_dev, b), F32),
            dma((2,)),
            dma((levels,)),
            dma((levels,)),
            dma((levels - 1,)),
            dma((levels,)),
            dma((levels - 1, CHUNKS)),
            dma((levels - 1, CHUNKS)),
            dma((n - 1,)),
            dma((n - 1,)),
            dma,
            dma((2, m - 1)),
            dma((2, m - 1)),
        ]
        + [pltpu.VMEM(coupling.shape[1:], BF16)] * (levels - 1),
        compiler_params=pltpu.CompilerParams(
            collective_id=0, has_side_effects=True, vmem_limit_bytes=56 * 1024 * 1024
        ),
    )(pattern, noise, diag, coupling)
    return pl.pallas_call(
        hand_out,
        out_shape=tuple(jax.ShapeDtypeStruct(a.shape, a.dtype) for a in solved),
        in_specs=[any_spec, any_spec],
        out_specs=(any_spec, any_spec),
        scratch_shapes=[
            pltpu.VMEM(solved[0].shape, BF16),
            pltpu.VMEM(solved[1].shape, F32),
            dma((levels,)),
            dma((levels,)),
            dma((2,)),
        ],
    )(*solved)


def solution(mesh):
    placed = (
        P(None, "rows", "samp", None),
        P(None, "rows", None, None),
        P(None, "rows", None, None, None),
        P(None, "rows", None),
    )
    return jax.shard_map(
        functools.partial(body, mesh.shape["rows"], mesh.shape["samp"]),
        mesh=mesh,
        in_specs=placed,
        out_specs=(P(None, "rows", "samp", None), P(None, "rows", None)),
        check_vma=False,
    )
```

```python
import functools

import jax
import jax.numpy as jnp
from jax import lax
from jax.experimental import pallas as pl
from jax.experimental.pallas import tpu as pltpu
from jax.sharding import PartitionSpec as P

MESH = pl.DeviceIdType.MESH
F32 = jnp.float32
BF16 = jnp.bfloat16
I32 = jnp.int32

CHUNKS = 2


def kernel(
    n, m, patv, noise_hbm, diag_hbm, coup_hbm,
    own, var_ref,
    pat, noise, diag, placed, table, send, recv,
    need, want_s, want_v, index_v, index, sums, vrecv,
    pat_sem, noise_sem, diag_sem, coup_sem, send_sem, recv_sem,
    nsend_sem, nrecv_sem, index_sem, vsend_sem, vrecv_sem, *coup,
):
    levels, slot_dev, samp, b = noise.shape
    fan = pat.shape[2]
    me = lax.axis_index("rows")
    q = lax.axis_index("samp")
    part = samp // CHUNKS
    order = list(range(n - 1, 0, -1))

    def partner(p):
        other, bit = me, 1
        while bit < n:
            if p & bit:
                other = other + bit - 2 * bit * lax.rem(lax.div(me, bit), 2)
            bit *= 2
        return other

    barrier = pltpu.get_barrier_semaphore()
    for p in order:
        pl.semaphore_signal(
            barrier, inc=1, device_id={"rows": partner(p)}, device_id_type=MESH
        )
    for o in range(1, m):
        pl.semaphore_signal(
            barrier, inc=1, device_id={"samp": lax.rem(q + o, m)}, device_id_type=MESH
        )

    def fetch(src, dst, sem, i):
        return pltpu.make_async_copy(src.at[i], dst.at[i], sem.at[i])

    def coup_fetch(i):
        return pltpu.make_async_copy(coup_hbm.at[i], coup[i], coup_sem.at[i])

    pat_copy = pltpu.make_async_copy(patv, pat, pat_sem)
    pat_copy.start()
    fetch(noise_hbm, noise, noise_sem, 0).start()
    fetch(diag_hbm, diag, diag_sem, 0).start()

    shape = (n, 8, fan)
    dev = lax.broadcasted_iota(I32, shape, 0)
    lev = lax.broadcasted_iota(I32, shape, 1)
    key = lev * n + dev
    best = jnp.zeros(shape, I32)
    for t in range(levels - 1):
        for s in range(slot_dev):
            entry = patv[t, s : s + 1, :].reshape(1, 1, fan)
            holder = lax.div(entry, jnp.int32(slot_dev))
            slot = entry - holder * slot_dev
            best = jnp.maximum(best, jnp.where(holder == key, slot, 0))
    best = jnp.broadcast_to(jnp.max(best, axis=2, keepdims=True), (n, 8, 128))
    row = lax.broadcasted_iota(I32, (n, 8, 128), 1)
    lane = lax.broadcasted_iota(I32, (n, 8, 128), 2)
    need[...] = jnp.sum(jnp.where(row == lane, best, 0), axis=1, keepdims=True)

    def need_copy(p):
        return pltpu.make_async_remote_copy(
            src_ref=need.at[partner(p)],
            dst_ref=want_v.at[p - 1],
            send_sem=nsend_sem.at[p - 1],
            recv_sem=nrecv_sem.at[p - 1],
            device_id={"rows": partner(p)},
            device_id_type=MESH,
        )

    def block_copy(level, h, p):
        return pltpu.make_async_remote_copy(
            src_ref=send.at[level, h, p - 1],
            dst_ref=recv.at[level, h, p - 1],
            send_sem=send_sem.at[level, h],
            recv_sem=recv_sem.at[level, h],
            device_id={"rows": partner(p)},
            device_id_type=MESH,
        )

    def chunk_copy(level, h):
        return pltpu.make_async_remote_copy(
            src_ref=send.at[level, h],
            dst_ref=recv.at[level, h],
            send_sem=send_sem.at[level, h],
            recv_sem=recv_sem.at[level, h],
            device_id={"rows": partner(1)},
            device_id_type=MESH,
        )

    def rest(level, s, h):
        residual = noise[level, s, pl.ds(h * part, part), :].astype(F32)
        total = None
        for k in range(0, fan, 2):
            picked = [
                table[h, lax.div(pat[level - 1, s, k + j], jnp.int32(slot_dev))]
                for j in range(2)
            ]
            term = jnp.dot(
                jnp.concatenate(picked, axis=1),
                coup[level - 1][s, pl.ds(k * b, 2 * b), :],
                preferred_element_type=F32,
            )
            total = term if total is None else total + term
        return (residual - total).astype(BF16)

    def finish(level, s, rounded):
        return jnp.dot(rounded, diag[level, s], preferred_element_type=F32).astype(BF16)

    def squares(x):
        wide = x.astype(F32)
        return jnp.sum(wide * wide, axis=0, keepdims=True)

    def receive(level, h):
        chunk_copy(level, h).wait_recv()
        for p in order:
            table[h, level * n + partner(p)] = recv[level, h, p - 1]

    pl.semaphore_wait(barrier, n - 1 + m - 1)
    for p in order:
        need_copy(p).start()
    for i in range(1, levels):
        fetch(noise_hbm, noise, noise_sem, i).start()
        fetch(diag_hbm, diag, diag_sem, i).start()
    coup_fetch(0).start()

    fetch(noise_hbm, noise, noise_sem, 0).wait()
    fetch(diag_hbm, diag, diag_sem, 0).wait()
    for s in range(slot_dev):
        x = jnp.dot(noise[0, s], diag[0, s], preferred_element_type=F32).astype(BF16)
        own[0, s] = x
        sums[0, pl.ds(s, 1), :] = squares(x)

    for p in order:
        need_copy(p).wait_recv()
    copy = pltpu.make_async_copy(want_v, want_s, index_sem)
    copy.start()
    copy.wait()
    for h in range(CHUNKS):
        for p in order:
            send[0, h, p - 1] = own[0, want_s[p - 1, 0, 0], pl.ds(h * part, part), :]
            block_copy(0, h, p).start()
    coup_fetch(1).start()

    mine = need[me]
    wants = [want_v[p - 1] for p in order] + [mine]
    slots = lax.broadcasted_iota(I32, (slot_dev, 128), 0)
    first = slots + n
    for i in range(n - 2, -1, -1):
        first = jnp.where(wants[i] == slots, i, first)
    rank = jnp.zeros((slot_dev, 128), I32)
    for s in range(slot_dev):
        rank = rank + (first[s : s + 1] < first).astype(I32)
    turn = jnp.zeros((slot_dev, 128), I32)
    for s in range(slot_dev):
        turn = turn + jnp.where(rank[s : s + 1] == slots, s, 0)
    index_v[pl.ds(0, slot_dev), :] = turn
    index_v[pl.ds(slot_dev, slot_dev), :] = rank
    for i in range(n):
        index_v[pl.ds(2 * slot_dev + i, 1), :] = jnp.sum(
            jnp.where(wants[i] == slots, rank, 0), axis=0, keepdims=True
        )
    index_v[pl.ds(2 * slot_dev + n, 1), :] = mine
    copy = pltpu.make_async_copy(index_v, index, index_sem)
    copy.start()
    copy.wait()
    pat_copy.wait()

    for h in range(CHUNKS):
        table[h, me] = own[0, index[2 * slot_dev + n, 0], pl.ds(h * part, part), :]
    for level in range(1, levels):
        fetch(noise_hbm, noise, noise_sem, level).wait()
        fetch(diag_hbm, diag, diag_sem, level).wait()

    for level in range(1, levels - 1):
        coup_fetch(level - 1).wait()
        for h in range(CHUNKS):
            rows = pl.ds(h * part, part)
            receive(level - 1, h)
            done = rest(level, index[0, level], h)
            for i in range(slot_dev):
                rounded = done
                if i + 1 < slot_dev:
                    done = rest(level, index[i + 1, level], h)
                placed[level - 1, i, rows, :] = finish(level, index[i, level], rounded)
                for j in range(i, min(i + 1, n - 1) if i + 1 < slot_dev else n - 1):
                    at = index[2 * slot_dev + j, level]
                    send[level, h, order[j] - 1] = placed[level - 1, at, rows, :]
                    block_copy(level, h, order[j]).start()
            if h == CHUNKS - 1 and level + 1 < levels - 1:
                coup_fetch(level + 1).start()
            table[h, level * n + me] = placed[
                level - 1, index[2 * slot_dev + n - 1, level], rows, :
            ]
        for s in range(slot_dev):
            x = placed[level - 1, index[slot_dev + s, level]]
            own[level, s] = x
            sums[level, pl.ds(s, 1), :] = squares(x)

    last = levels - 1

    def var_copy(o, i):
        at = (pl.ds(0, last), pl.ds(last, 1))[i]
        return pltpu.make_async_remote_copy(
            src_ref=sums.at[at],
            dst_ref=vrecv.at[o - 1, at],
            send_sem=vsend_sem.at[i, o - 1],
            recv_sem=vrecv_sem.at[i, o - 1],
            device_id={"samp": lax.rem(q + o, m)},
            device_id_type=MESH,
        )

    for o in range(1, m):
        var_copy(o, 0).start()
    coup_fetch(last - 1).wait()
    for h in range(CHUNKS):
        rows = pl.ds(h * part, part)
        receive(last - 1, h)
        for s in range(slot_dev):
            x = finish(last, s, rest(last, s, h))
            own[last, s, rows, :] = x
            found = squares(x)
            if h > 0:
                found = found + sums[last, pl.ds(s, 1), :]
            sums[last, pl.ds(s, 1), :] = found
    for o in range(1, m):
        var_copy(o, 1).start()
    for level in range(levels - 1):
        for h in range(CHUNKS):
            chunk_copy(level, h).wait_send()
    for p in order:
        need_copy(p).wait_send()
    for i in range(2):
        for o in range(1, m):
            var_copy(o, i).wait()
    total = sums[...]
    for o in range(1, m):
        total = total + vrecv[o - 1]
    var_ref[...] = total * (1.0 / (samp * m))


def hand_out(x, v, y_hbm, w_hbm, sem):
    copies = [
        pltpu.make_async_copy(x, y_hbm, sem.at[0]),
        pltpu.make_async_copy(v, w_hbm, sem.at[1]),
    ]
    for copy in copies:
        copy.start()
    for copy in copies:
        copy.wait()


def body(n, m, noise, diag, coupling, pattern):
    levels, slot_dev, samp, b = noise.shape
    fan = coupling.shape[2]
    part = samp // CHUNKS
    any_spec = pl.BlockSpec(memory_space=pl.ANY)
    vmem_spec = pl.BlockSpec(memory_space=pltpu.VMEM)
    dma = pltpu.SemaphoreType.DMA
    coupling = coupling.reshape(levels - 1, slot_dev, fan * b, b)
    lines = 2 * slot_dev + -(-(n + 1) // 8) * 8
    solved = pl.pallas_call(
        functools.partial(kernel, n, m),
        out_shape=(
            jax.ShapeDtypeStruct(noise.shape, BF16),
            jax.ShapeDtypeStruct((levels, slot_dev, b), F32),
        ),
        in_specs=[vmem_spec, any_spec, any_spec, any_spec],
        out_specs=(vmem_spec, vmem_spec),
        scratch_shapes=[
            pltpu.SMEM(pattern.shape, I32),
            pltpu.VMEM(noise.shape, BF16),
            pltpu.VMEM(diag.shape, BF16),
            pltpu.VMEM((levels - 2, slot_dev, samp, b), BF16),
            pltpu.VMEM((CHUNKS, (levels - 1) * n, part, b), BF16),
            pltpu.VMEM((levels - 1, CHUNKS, n - 1, part, b), BF16),
            pltpu.VMEM((levels - 1, CHUNKS, n - 1, part, b), BF16),
            pltpu.VMEM((n, 1, 128), I32),
            pltpu.SMEM((n - 1, 1, 128), I32),
            pltpu.VMEM((n - 1, 1, 128), I32),
            pltpu.VMEM((lines, 128), I32),
            pltpu.SMEM((lines, 128), I32),
            pltpu.VMEM((levels, slot_dev, b), F32),
            pltpu.VMEM((m - 1, levels, slot_dev, b), F32),
            dma,
            dma((levels,)),
            dma((levels,)),
            dma((levels - 1,)),
            dma((levels - 1, CHUNKS)),
            dma((levels - 1, CHUNKS)),
            dma((n - 1,)),
            dma((n - 1,)),
            dma,
            dma((2, m - 1)),
            dma((2, m - 1)),
        ]
        + [pltpu.VMEM(coupling.shape[1:], BF16)] * (levels - 1),
        compiler_params=pltpu.CompilerParams(
            collective_id=0, has_side_effects=True, vmem_limit_bytes=54935552
        ),
    )(pattern, noise, diag, coupling)
    return pl.pallas_call(
        hand_out,
        out_shape=tuple(jax.ShapeDtypeStruct(a.shape, a.dtype) for a in solved),
        in_specs=[any_spec, any_spec],
        out_specs=(any_spec, any_spec),
        scratch_shapes=[dma((2,))],
        compiler_params=pltpu.CompilerParams(vmem_limit_bytes=8 * 1024 * 1024),
    )(*solved)


def solution(mesh):
    placed = (
        P(None, "rows", "samp", None),
        P(None, "rows", None, None),
        P(None, "rows", None, None, None),
        P(None, "rows", None),
    )
    return jax.shard_map(
        functools.partial(body, mesh.shape["rows"], mesh.shape["samp"]),
        mesh=mesh,
        in_specs=placed,
        out_specs=(P(None, "rows", "samp", None), P(None, "rows", None)),
        check_vma=False,
    )
```

```python
import functools

import jax
import jax.numpy as jnp
from jax import lax
from jax.experimental import pallas as pl
from jax.experimental.pallas import tpu as pltpu
from jax.sharding import PartitionSpec as P

MESH = pl.DeviceIdType.MESH
F32 = jnp.float32
BF16 = jnp.bfloat16
I32 = jnp.int32

CHUNKS = 2


def kernel(
    n, m, patv, noise_hbm, diag_hbm, coup_hbm,
    own, var_ref,
    pat, noise, diag, placed, table, send, recv,
    need, want_v, index_v, index, sums, vrecv,
    pat_sem, noise_sem, diag_sem, coup_sem, send_sem, recv_sem,
    nsend_sem, nrecv_sem, index_sem, vsend_sem, vrecv_sem, *coup,
):
    levels, slot_dev, samp, b = noise.shape
    fan = pat.shape[2]
    me = lax.axis_index("rows")
    q = lax.axis_index("samp")
    part = samp // CHUNKS
    order = list(range(n - 1, 0, -1))

    def partner(p):
        other, bit = me, 1
        while bit < n:
            if p & bit:
                other = other + bit - 2 * bit * lax.rem(lax.div(me, bit), 2)
            bit *= 2
        return other

    barrier = pltpu.get_barrier_semaphore()
    for p in order:
        pl.semaphore_signal(
            barrier, inc=1, device_id={"rows": partner(p)}, device_id_type=MESH
        )
    for o in range(1, m):
        pl.semaphore_signal(
            barrier, inc=1, device_id={"samp": lax.rem(q + o, m)}, device_id_type=MESH
        )

    def fetch(src, dst, sem, i):
        return pltpu.make_async_copy(src.at[i], dst.at[i], sem.at[i])

    def coup_fetch(i):
        return pltpu.make_async_copy(coup_hbm.at[i], coup[i], coup_sem.at[i])

    pat_copy = pltpu.make_async_copy(patv, pat, pat_sem)
    pat_copy.start()
    fetch(noise_hbm, noise, noise_sem, 0).start()
    fetch(diag_hbm, diag, diag_sem, 0).start()

    shape = (n, 8, fan)
    dev = lax.broadcasted_iota(I32, shape, 0)
    lev = lax.broadcasted_iota(I32, shape, 1)
    key = lev * n + dev
    best = jnp.zeros(shape, I32)
    for t in range(levels - 1):
        for s in range(slot_dev):
            entry = patv[t, s : s + 1, :].reshape(1, 1, fan)
            holder = lax.div(entry, jnp.int32(slot_dev))
            slot = entry - holder * slot_dev
            best = jnp.maximum(best, jnp.where(holder == key, slot, 0))
    best = jnp.broadcast_to(jnp.max(best, axis=2, keepdims=True), (n, 8, 128))
    row = lax.broadcasted_iota(I32, (n, 8, 128), 1)
    lane = lax.broadcasted_iota(I32, (n, 8, 128), 2)
    need[...] = jnp.sum(jnp.where(row == lane, best, 0), axis=1, keepdims=True)

    def need_copy(p):
        return pltpu.make_async_remote_copy(
            src_ref=need.at[partner(p)],
            dst_ref=want_v.at[p - 1],
            send_sem=nsend_sem.at[p - 1],
            recv_sem=nrecv_sem.at[p - 1],
            device_id={"rows": partner(p)},
            device_id_type=MESH,
        )

    def block_copy(level, h, p):
        return pltpu.make_async_remote_copy(
            src_ref=send.at[level, h, p - 1],
            dst_ref=recv.at[level, h, p - 1],
            send_sem=send_sem.at[level, h],
            recv_sem=recv_sem.at[level, h],
            device_id={"rows": partner(p)},
            device_id_type=MESH,
        )

    def chunk_copy(level, h):
        return pltpu.make_async_remote_copy(
            src_ref=send.at[level, h],
            dst_ref=recv.at[level, h],
            send_sem=send_sem.at[level, h],
            recv_sem=recv_sem.at[level, h],
            device_id={"rows": partner(1)},
            device_id_type=MESH,
        )

    def rest(level, s, h):
        residual = noise[level, s, pl.ds(h * part, part), :].astype(F32)
        total = None
        for k in range(0, fan, 2):
            picked = [
                table[h, lax.div(pat[level - 1, s, k + j], jnp.int32(slot_dev))]
                for j in range(2)
            ]
            term = jnp.dot(
                jnp.concatenate(picked, axis=1),
                coup[level - 1][s, pl.ds(k * b, 2 * b), :],
                preferred_element_type=F32,
            )
            total = term if total is None else total + term
        return (residual - total).astype(BF16)

    def finish(level, s, rounded):
        return jnp.dot(rounded, diag[level, s], preferred_element_type=F32).astype(BF16)

    def squares(x):
        wide = x.astype(F32)
        return jnp.sum(wide * wide, axis=0, keepdims=True)

    def receive(level, h):
        chunk_copy(level, h).wait_recv()
        for p in order:
            table[h, level * n + partner(p)] = recv[level, h, p - 1]

    pl.semaphore_wait(barrier, n - 1 + m - 1)
    for p in order:
        need_copy(p).start()
    for i in range(1, levels):
        fetch(noise_hbm, noise, noise_sem, i).start()
        fetch(diag_hbm, diag, diag_sem, i).start()
    coup_fetch(0).start()

    fetch(noise_hbm, noise, noise_sem, 0).wait()
    fetch(diag_hbm, diag, diag_sem, 0).wait()
    for s in range(slot_dev):
        x = jnp.dot(noise[0, s], diag[0, s], preferred_element_type=F32).astype(BF16)
        own[0, s] = x
        sums[0, pl.ds(s, 1), :] = squares(x)

    for p in order:
        need_copy(p).wait_recv()
        block = own[0, want_v[p - 1][0, 0]]
        for h in range(CHUNKS):
            send[0, h, p - 1] = block[h * part : (h + 1) * part]
        block_copy(0, 0, p).start()
    for h in range(1, CHUNKS):
        for p in order:
            block_copy(0, h, p).start()
    coup_fetch(1).start()

    mine = need[me]
    wants = [want_v[p - 1] for p in order] + [mine]
    slots = lax.broadcasted_iota(I32, (slot_dev, 128), 0)
    first = slots + n
    for i in range(n - 2, -1, -1):
        first = jnp.where(wants[i] == slots, i, first)
    rank = jnp.zeros((slot_dev, 128), I32)
    for s in range(slot_dev):
        rank = rank + (first[s : s + 1] < first).astype(I32)
    turn = jnp.zeros((slot_dev, 128), I32)
    for s in range(slot_dev):
        turn = turn + jnp.where(rank[s : s + 1] == slots, s, 0)
    index_v[pl.ds(0, slot_dev), :] = turn
    index_v[pl.ds(slot_dev, slot_dev), :] = rank
    for i in range(n):
        index_v[pl.ds(2 * slot_dev + i, 1), :] = jnp.sum(
            jnp.where(wants[i] == slots, rank, 0), axis=0, keepdims=True
        )
    index_v[pl.ds(2 * slot_dev + n, 1), :] = mine
    copy = pltpu.make_async_copy(index_v, index, index_sem)
    copy.start()
    copy.wait()
    pat_copy.wait()

    for h in range(CHUNKS):
        table[h, me] = own[0, index[2 * slot_dev + n, 0], pl.ds(h * part, part), :]
    for level in range(1, levels):
        fetch(noise_hbm, noise, noise_sem, level).wait()
        fetch(diag_hbm, diag, diag_sem, level).wait()

    for level in range(1, levels - 1):
        coup_fetch(level - 1).wait()
        for h in range(CHUNKS):
            rows = pl.ds(h * part, part)
            receive(level - 1, h)
            done = rest(level, index[0, level], h)
            for i in range(slot_dev):
                rounded = done
                if i + 1 < slot_dev:
                    done = rest(level, index[i + 1, level], h)
                placed[level - 1, i, rows, :] = finish(level, index[i, level], rounded)
                for j in range(i, min(i + 1, n - 1) if i + 1 < slot_dev else n - 1):
                    at = index[2 * slot_dev + j, level]
                    send[level, h, order[j] - 1] = placed[level - 1, at, rows, :]
                    block_copy(level, h, order[j]).start()
            if h == CHUNKS - 1 and level + 1 < levels - 1:
                coup_fetch(level + 1).start()
            table[h, level * n + me] = placed[
                level - 1, index[2 * slot_dev + n - 1, level], rows, :
            ]
        for s in range(slot_dev):
            x = placed[level - 1, index[slot_dev + s, level]]
            own[level, s] = x
            sums[level, pl.ds(s, 1), :] = squares(x)

    last = levels - 1

    def var_copy(o, i):
        at = (pl.ds(0, last), pl.ds(last, 1))[i]
        return pltpu.make_async_remote_copy(
            src_ref=sums.at[at],
            dst_ref=vrecv.at[o - 1, at],
            send_sem=vsend_sem.at[i, o - 1],
            recv_sem=vrecv_sem.at[i, o - 1],
            device_id={"samp": lax.rem(q + o, m)},
            device_id_type=MESH,
        )

    for o in range(1, m):
        var_copy(o, 0).start()
    coup_fetch(last - 1).wait()
    for h in range(CHUNKS):
        rows = pl.ds(h * part, part)
        receive(last - 1, h)
        for s in range(slot_dev):
            x = finish(last, s, rest(last, s, h))
            own[last, s, rows, :] = x
            found = squares(x)
            if h > 0:
                found = found + sums[last, pl.ds(s, 1), :]
            sums[last, pl.ds(s, 1), :] = found
    for o in range(1, m):
        var_copy(o, 1).start()
    for level in range(levels - 1):
        for h in range(CHUNKS):
            chunk_copy(level, h).wait_send()
    for p in order:
        need_copy(p).wait_send()
    for i in range(2):
        for o in range(1, m):
            var_copy(o, i).wait()
    total = sums[...]
    for o in range(1, m):
        total = total + vrecv[o - 1]
    var_ref[...] = total * (1.0 / (samp * m))


def hand_out(x, v, y_hbm, w_hbm, sem):
    copies = [
        pltpu.make_async_copy(x, y_hbm, sem.at[0]),
        pltpu.make_async_copy(v, w_hbm, sem.at[1]),
    ]
    for copy in copies:
        copy.start()
    for copy in copies:
        copy.wait()


def body(n, m, noise, diag, coupling, pattern):
    levels, slot_dev, samp, b = noise.shape
    fan = coupling.shape[2]
    part = samp // CHUNKS
    any_spec = pl.BlockSpec(memory_space=pl.ANY)
    vmem_spec = pl.BlockSpec(memory_space=pltpu.VMEM)
    dma = pltpu.SemaphoreType.DMA
    coupling = coupling.reshape(levels - 1, slot_dev, fan * b, b)
    lines = 2 * slot_dev + -(-(n + 1) // 8) * 8
    solved = pl.pallas_call(
        functools.partial(kernel, n, m),
        out_shape=(
            jax.ShapeDtypeStruct(noise.shape, BF16),
            jax.ShapeDtypeStruct((levels, slot_dev, b), F32),
        ),
        in_specs=[vmem_spec, any_spec, any_spec, any_spec],
        out_specs=(vmem_spec, vmem_spec),
        scratch_shapes=[
            pltpu.SMEM(pattern.shape, I32),
            pltpu.VMEM(noise.shape, BF16),
            pltpu.VMEM(diag.shape, BF16),
            pltpu.VMEM((levels - 2, slot_dev, samp, b), BF16),
            pltpu.VMEM((CHUNKS, (levels - 1) * n, part, b), BF16),
            pltpu.VMEM((levels - 1, CHUNKS, n - 1, part, b), BF16),
            pltpu.VMEM((levels - 1, CHUNKS, n - 1, part, b), BF16),
            pltpu.VMEM((n, 1, 128), I32),
            pltpu.VMEM((n - 1, 1, 128), I32),
            pltpu.VMEM((lines, 128), I32),
            pltpu.SMEM((lines, 128), I32),
            pltpu.VMEM((levels, slot_dev, b), F32),
            pltpu.VMEM((m - 1, levels, slot_dev, b), F32),
            dma,
            dma((levels,)),
            dma((levels,)),
            dma((levels - 1,)),
            dma((levels - 1, CHUNKS)),
            dma((levels - 1, CHUNKS)),
            dma((n - 1,)),
            dma((n - 1,)),
            dma,
            dma((2, m - 1)),
            dma((2, m - 1)),
        ]
        + [pltpu.VMEM(coupling.shape[1:], BF16)] * (levels - 1),
        compiler_params=pltpu.CompilerParams(
            collective_id=0, has_side_effects=True, vmem_limit_bytes=48 * 1024 * 1024
        ),
    )(pattern, *(pltpu.with_memory_space_constraint(a, pltpu.HBM) for a in (noise, diag, coupling)))
    return pl.pallas_call(
        hand_out,
        out_shape=tuple(jax.ShapeDtypeStruct(a.shape, a.dtype) for a in solved),
        in_specs=[any_spec, any_spec],
        out_specs=(any_spec, any_spec),
        scratch_shapes=[dma((2,))],
        compiler_params=pltpu.CompilerParams(vmem_limit_bytes=8 * 1024 * 1024),
    )(*solved)


def solution(mesh):
    placed = (
        P(None, "rows", "samp", None),
        P(None, "rows", None, None),
        P(None, "rows", None, None, None),
        P(None, "rows", None),
    )
    return jax.shard_map(
        functools.partial(body, mesh.shape["rows"], mesh.shape["samp"]),
        mesh=mesh,
        in_specs=placed,
        out_specs=(P(None, "rows", "samp", None), P(None, "rows", None)),
        check_vma=False,
    )
```

```python
import functools

import jax
import jax.numpy as jnp
from jax import lax
from jax.experimental import pallas as pl
from jax.experimental.pallas import tpu as pltpu
from jax.sharding import PartitionSpec as P

MESH = pl.DeviceIdType.MESH
F32 = jnp.float32
BF16 = jnp.bfloat16
I32 = jnp.int32

CHUNKS = 2


def kernel(
    n, m, pat_hbm, noise_hbm, diag_hbm, coup_hbm,
    own, var_ref,
    pat, patv, noise, diag, placed, table, send, recv,
    need, want_v, index_v, index, sums, vrecv,
    pat_sem, noise_sem, diag_sem, coup_sem, send_sem, recv_sem,
    nsend_sem, nrecv_sem, index_sem, vsend_sem, vrecv_sem, *coup,
):
    levels, slot_dev, samp, b = noise.shape
    fan = pat.shape[2]
    me = lax.axis_index("rows")
    q = lax.axis_index("samp")
    part = samp // CHUNKS
    order = list(range(n - 1, 0, -1))

    def partner(p):
        other, bit = me, 1
        while bit < n:
            if p & bit:
                other = other + bit - 2 * bit * lax.rem(lax.div(me, bit), 2)
            bit *= 2
        return other

    barrier = pltpu.get_barrier_semaphore()
    for p in order:
        pl.semaphore_signal(
            barrier, inc=1, device_id={"rows": partner(p)}, device_id_type=MESH
        )
    for o in range(1, m):
        pl.semaphore_signal(
            barrier, inc=1, device_id={"samp": lax.rem(q + o, m)}, device_id_type=MESH
        )

    def fetch(src, dst, sem, i):
        return pltpu.make_async_copy(src.at[i], dst.at[i], sem.at[i])

    def coup_fetch(i):
        return pltpu.make_async_copy(coup_hbm.at[i], coup[i], coup_sem.at[i])

    patv_copy = pltpu.make_async_copy(pat_hbm, patv, pat_sem.at[0])
    patv_copy.start()
    fetch(noise_hbm, noise, noise_sem, 0).start()
    fetch(diag_hbm, diag, diag_sem, 0).start()

    patv_copy.wait()
    pat_copy = pltpu.make_async_copy(patv, pat, pat_sem.at[1])
    pat_copy.start()
    shape = (n, 8, fan)
    dev = lax.broadcasted_iota(I32, shape, 0)
    lev = lax.broadcasted_iota(I32, shape, 1)
    key = lev * n + dev
    best = jnp.zeros(shape, I32)
    for t in range(levels - 1):
        for s in range(slot_dev):
            entry = patv[t, s : s + 1, :].reshape(1, 1, fan)
            holder = lax.div(entry, jnp.int32(slot_dev))
            slot = entry - holder * slot_dev
            best = jnp.maximum(best, jnp.where(holder == key, slot, 0))
    best = jnp.broadcast_to(jnp.max(best, axis=2, keepdims=True), (n, 8, 128))
    row = lax.broadcasted_iota(I32, (n, 8, 128), 1)
    lane = lax.broadcasted_iota(I32, (n, 8, 128), 2)
    need[...] = jnp.sum(jnp.where(row == lane, best, 0), axis=1, keepdims=True)

    def need_copy(p):
        return pltpu.make_async_remote_copy(
            src_ref=need.at[partner(p)],
            dst_ref=want_v.at[p - 1],
            send_sem=nsend_sem.at[p - 1],
            recv_sem=nrecv_sem.at[p - 1],
            device_id={"rows": partner(p)},
            device_id_type=MESH,
        )

    def block_copy(level, h, p):
        return pltpu.make_async_remote_copy(
            src_ref=send.at[level, h, p - 1],
            dst_ref=recv.at[level, h, p - 1],
            send_sem=send_sem.at[level, h],
            recv_sem=recv_sem.at[level, h],
            device_id={"rows": partner(p)},
            device_id_type=MESH,
        )

    def chunk_copy(level, h):
        return pltpu.make_async_remote_copy(
            src_ref=send.at[level, h],
            dst_ref=recv.at[level, h],
            send_sem=send_sem.at[level, h],
            recv_sem=recv_sem.at[level, h],
            device_id={"rows": partner(1)},
            device_id_type=MESH,
        )

    def rest(level, s, h):
        residual = noise[level, s, pl.ds(h * part, part), :].astype(F32)
        total = None
        for k in range(0, fan, 2):
            picked = [
                table[h, lax.div(pat[level - 1, s, k + j], jnp.int32(slot_dev))]
                for j in range(2)
            ]
            term = jnp.dot(
                jnp.concatenate(picked, axis=1),
                coup[level - 1][s, pl.ds(k * b, 2 * b), :],
                preferred_element_type=F32,
            )
            total = term if total is None else total + term
        return (residual - total).astype(BF16)

    def finish(level, s, rounded):
        return jnp.dot(rounded, diag[level, s], preferred_element_type=F32).astype(BF16)

    def squares(x):
        wide = x.astype(F32)
        return jnp.sum(wide * wide, axis=0, keepdims=True)

    def receive(level, h):
        chunk_copy(level, h).wait_recv()
        for p in order:
            table[h, level * n + partner(p)] = recv[level, h, p - 1]

    pl.semaphore_wait(barrier, n - 1 + m - 1)
    for p in order:
        need_copy(p).start()
    for i in range(1, levels):
        fetch(noise_hbm, noise, noise_sem, i).start()
        fetch(diag_hbm, diag, diag_sem, i).start()
    coup_fetch(0).start()

    fetch(noise_hbm, noise, noise_sem, 0).wait()
    fetch(diag_hbm, diag, diag_sem, 0).wait()
    for s in range(slot_dev):
        x = jnp.dot(noise[0, s], diag[0, s], preferred_element_type=F32).astype(BF16)
        own[0, s] = x
        sums[0, pl.ds(s, 1), :] = squares(x)

    for p in order:
        need_copy(p).wait_recv()
        block = own[0, want_v[p - 1][0, 0]]
        for h in range(CHUNKS):
            send[0, h, p - 1] = block[h * part : (h + 1) * part]
        block_copy(0, 0, p).start()
    for h in range(1, CHUNKS):
        for p in order:
            block_copy(0, h, p).start()
    coup_fetch(1).start()

    mine = need[me]
    wants = [want_v[p - 1] for p in order] + [mine]
    slots = lax.broadcasted_iota(I32, (slot_dev, 128), 0)
    first = slots + n
    for i in range(n - 2, -1, -1):
        first = jnp.where(wants[i] == slots, i, first)
    rank = jnp.zeros((slot_dev, 128), I32)
    for s in range(slot_dev):
        rank = rank + (first[s : s + 1] < first).astype(I32)
    turn = jnp.zeros((slot_dev, 128), I32)
    for s in range(slot_dev):
        turn = turn + jnp.where(rank[s : s + 1] == slots, s, 0)
    index_v[pl.ds(0, slot_dev), :] = turn
    index_v[pl.ds(slot_dev, slot_dev), :] = rank
    for i in range(n):
        index_v[pl.ds(2 * slot_dev + i, 1), :] = jnp.sum(
            jnp.where(wants[i] == slots, rank, 0), axis=0, keepdims=True
        )
    index_v[pl.ds(2 * slot_dev + n, 1), :] = mine
    copy = pltpu.make_async_copy(index_v, index, index_sem)
    copy.start()
    copy.wait()
    pat_copy.wait()

    for h in range(CHUNKS):
        table[h, me] = own[0, index[2 * slot_dev + n, 0], pl.ds(h * part, part), :]
    for level in range(1, levels):
        fetch(noise_hbm, noise, noise_sem, level).wait()
        fetch(diag_hbm, diag, diag_sem, level).wait()

    for level in range(1, levels - 1):
        coup_fetch(level - 1).wait()
        for h in range(CHUNKS):
            rows = pl.ds(h * part, part)
            receive(level - 1, h)
            done = rest(level, index[0, level], h)
            for i in range(slot_dev):
                rounded = done
                if i + 1 < slot_dev:
                    done = rest(level, index[i + 1, level], h)
                placed[level - 1, i, rows, :] = finish(level, index[i, level], rounded)
                for j in range(i, min(i + 1, n - 1) if i + 1 < slot_dev else n - 1):
                    at = index[2 * slot_dev + j, level]
                    send[level, h, order[j] - 1] = placed[level - 1, at, rows, :]
                    block_copy(level, h, order[j]).start()
            if h == CHUNKS - 1 and level + 1 < levels - 1:
                coup_fetch(level + 1).start()
            table[h, level * n + me] = placed[
                level - 1, index[2 * slot_dev + n - 1, level], rows, :
            ]
        for s in range(slot_dev):
            x = placed[level - 1, index[slot_dev + s, level]]
            own[level, s] = x
            sums[level, pl.ds(s, 1), :] = squares(x)

    last = levels - 1

    def var_copy(o, i):
        at = (pl.ds(0, last), pl.ds(last, 1))[i]
        return pltpu.make_async_remote_copy(
            src_ref=sums.at[at],
            dst_ref=vrecv.at[o - 1, at],
            send_sem=vsend_sem.at[i, o - 1],
            recv_sem=vrecv_sem.at[i, o - 1],
            device_id={"samp": lax.rem(q + o, m)},
            device_id_type=MESH,
        )

    for o in range(1, m):
        var_copy(o, 0).start()
    coup_fetch(last - 1).wait()
    for h in range(CHUNKS):
        rows = pl.ds(h * part, part)
        receive(last - 1, h)
        for s in range(slot_dev):
            x = finish(last, s, rest(last, s, h))
            own[last, s, rows, :] = x
            found = squares(x)
            if h > 0:
                found = found + sums[last, pl.ds(s, 1), :]
            sums[last, pl.ds(s, 1), :] = found
    for o in range(1, m):
        var_copy(o, 1).start()
    for level in range(levels - 1):
        for h in range(CHUNKS):
            chunk_copy(level, h).wait_send()
    for p in order:
        need_copy(p).wait_send()
    for i in range(2):
        for o in range(1, m):
            var_copy(o, i).wait()
    total = sums[...]
    for o in range(1, m):
        total = total + vrecv[o - 1]
    var_ref[...] = total * (1.0 / (samp * m))


def hand_out(x, v, y_hbm, w_hbm, sem):
    copies = [
        pltpu.make_async_copy(x, y_hbm, sem.at[0]),
        pltpu.make_async_copy(v, w_hbm, sem.at[1]),
    ]
    for copy in copies:
        copy.start()
    for copy in copies:
        copy.wait()


def body(n, m, noise, diag, coupling, pattern):
    levels, slot_dev, samp, b = noise.shape
    fan = coupling.shape[2]
    part = samp // CHUNKS
    any_spec = pl.BlockSpec(memory_space=pl.ANY)
    vmem_spec = pl.BlockSpec(memory_space=pltpu.VMEM)
    dma = pltpu.SemaphoreType.DMA
    coupling = coupling.reshape(levels - 1, slot_dev, fan * b, b)
    lines = 2 * slot_dev + -(-(n + 1) // 8) * 8
    solved = pl.pallas_call(
        functools.partial(kernel, n, m),
        out_shape=(
            jax.ShapeDtypeStruct(noise.shape, BF16),
            jax.ShapeDtypeStruct((levels, slot_dev, b), F32),
        ),
        in_specs=[any_spec] * 4,
        out_specs=(vmem_spec, vmem_spec),
        scratch_shapes=[
            pltpu.SMEM(pattern.shape, I32),
            pltpu.VMEM(pattern.shape, I32),
            pltpu.VMEM(noise.shape, BF16),
            pltpu.VMEM(diag.shape, BF16),
            pltpu.VMEM((levels - 2, slot_dev, samp, b), BF16),
            pltpu.VMEM((CHUNKS, (levels - 1) * n, part, b), BF16),
            pltpu.VMEM((levels - 1, CHUNKS, n - 1, part, b), BF16),
            pltpu.VMEM((levels - 1, CHUNKS, n - 1, part, b), BF16),
            pltpu.VMEM((n, 1, 128), I32),
            pltpu.VMEM((n - 1, 1, 128), I32),
            pltpu.VMEM((lines, 128), I32),
            pltpu.SMEM((lines, 128), I32),
            pltpu.VMEM((levels, slot_dev, b), F32),
            pltpu.VMEM((m - 1, levels, slot_dev, b), F32),
            dma((2,)),
            dma((levels,)),
            dma((levels,)),
            dma((levels - 1,)),
            dma((levels - 1, CHUNKS)),
            dma((levels - 1, CHUNKS)),
            dma((n - 1,)),
            dma((n - 1,)),
            dma,
            dma((2, m - 1)),
            dma((2, m - 1)),
        ]
        + [pltpu.VMEM(coupling.shape[1:], BF16)] * (levels - 1),
        compiler_params=pltpu.CompilerParams(
            collective_id=0, has_side_effects=True, vmem_limit_bytes=48 * 1024 * 1024
        ),
    )(*(pltpu.with_memory_space_constraint(a, pltpu.HBM) for a in (pattern, noise, diag, coupling)))
    return pl.pallas_call(
        hand_out,
        out_shape=tuple(jax.ShapeDtypeStruct(a.shape, a.dtype) for a in solved),
        in_specs=[any_spec, any_spec],
        out_specs=(any_spec, any_spec),
        scratch_shapes=[dma((2,))],
        compiler_params=pltpu.CompilerParams(vmem_limit_bytes=8 * 1024 * 1024),
    )(*solved)


def solution(mesh):
    placed = (
        P(None, "rows", "samp", None),
        P(None, "rows", None, None),
        P(None, "rows", None, None, None),
        P(None, "rows", None),
    )
    return jax.shard_map(
        functools.partial(body, mesh.shape["rows"], mesh.shape["samp"]),
        mesh=mesh,
        in_specs=placed,
        out_specs=(P(None, "rows", "samp", None), P(None, "rows", None)),
        check_vma=False,
    )
```

```python
import functools

import jax
import jax.numpy as jnp
from jax import lax
from jax.experimental import pallas as pl
from jax.experimental.pallas import tpu as pltpu
from jax.sharding import PartitionSpec as P

MESH = pl.DeviceIdType.MESH
F32 = jnp.float32
BF16 = jnp.bfloat16
I32 = jnp.int32

CHUNKS = 2


def kernel(
    n, m, pat_hbm, noise_hbm, diag_hbm, coup_hbm,
    own, var_ref,
    pat, patv, noise, diag, placed, table, send, recv,
    need, want_v, index_v, index, sums, vrecv,
    pat_sem, noise_sem, diag_sem, coup_sem, send_sem, recv_sem,
    nsend_sem, nrecv_sem, index_sem, vsend_sem, vrecv_sem, *coup,
):
    levels, slot_dev, samp, b = noise.shape
    fan = pat.shape[2]
    me = lax.axis_index("rows")
    q = lax.axis_index("samp")
    part = samp // CHUNKS
    order = list(range(n - 1, 0, -1))

    def partner(p):
        other, bit = me, 1
        while bit < n:
            if p & bit:
                other = other + bit - 2 * bit * lax.rem(lax.div(me, bit), 2)
            bit *= 2
        return other

    barrier = pltpu.get_barrier_semaphore()
    for p in order:
        pl.semaphore_signal(
            barrier, inc=1, device_id={"rows": partner(p)}, device_id_type=MESH
        )
    for o in range(1, m):
        pl.semaphore_signal(
            barrier, inc=1, device_id={"samp": lax.rem(q + o, m)}, device_id_type=MESH
        )

    def fetch(src, dst, sem, i):
        return pltpu.make_async_copy(src.at[i], dst.at[i], sem.at[i])

    def coup_fetch(i):
        return pltpu.make_async_copy(coup_hbm.at[i], coup[i], coup_sem.at[i])

    patv_copy = pltpu.make_async_copy(pat_hbm, patv, pat_sem.at[0])
    patv_copy.start()
    fetch(noise_hbm, noise, noise_sem, 0).start()
    fetch(diag_hbm, diag, diag_sem, 0).start()

    patv_copy.wait()
    pat_copy = pltpu.make_async_copy(patv, pat, pat_sem.at[1])
    pat_copy.start()
    shape = (n, 8, fan)
    dev = lax.broadcasted_iota(I32, shape, 0)
    lev = lax.broadcasted_iota(I32, shape, 1)
    key = lev * n + dev
    best = jnp.zeros(shape, I32)
    for t in range(levels - 1):
        for s in range(slot_dev):
            entry = patv[t, s : s + 1, :].reshape(1, 1, fan)
            holder = lax.div(entry, jnp.int32(slot_dev))
            slot = entry - holder * slot_dev
            best = jnp.maximum(best, jnp.where(holder == key, slot, 0))
    best = jnp.broadcast_to(jnp.max(best, axis=2, keepdims=True), (n, 8, 128))
    row = lax.broadcasted_iota(I32, (n, 8, 128), 1)
    lane = lax.broadcasted_iota(I32, (n, 8, 128), 2)
    need[...] = jnp.sum(jnp.where(row == lane, best, 0), axis=1, keepdims=True)

    def need_copy(p):
        return pltpu.make_async_remote_copy(
            src_ref=need.at[partner(p)],
            dst_ref=want_v.at[p - 1],
            send_sem=nsend_sem.at[p - 1],
            recv_sem=nrecv_sem.at[p - 1],
            device_id={"rows": partner(p)},
            device_id_type=MESH,
        )

    def block_copy(level, h, p):
        return pltpu.make_async_remote_copy(
            src_ref=send.at[level, h, p - 1],
            dst_ref=recv.at[level, h, p - 1],
            send_sem=send_sem.at[level, h],
            recv_sem=recv_sem.at[level, h],
            device_id={"rows": partner(p)},
            device_id_type=MESH,
        )

    def chunk_copy(level, h):
        return pltpu.make_async_remote_copy(
            src_ref=send.at[level, h],
            dst_ref=recv.at[level, h],
            send_sem=send_sem.at[level, h],
            recv_sem=recv_sem.at[level, h],
            device_id={"rows": partner(1)},
            device_id_type=MESH,
        )

    def rest(level, s, h):
        residual = noise[level, s, pl.ds(h * part, part), :].astype(F32)
        total = None
        for k in range(0, fan, 2):
            picked = [
                table[h, lax.div(pat[level - 1, s, k + j], jnp.int32(slot_dev))]
                for j in range(2)
            ]
            term = jnp.dot(
                jnp.concatenate(picked, axis=1),
                coup[level - 1][s, pl.ds(k * b, 2 * b), :],
                preferred_element_type=F32,
            )
            total = term if total is None else total + term
        return (residual - total).astype(BF16)

    def finish(level, s, rounded):
        return jnp.dot(rounded, diag[level, s], preferred_element_type=F32).astype(BF16)

    def squares(x):
        wide = x.astype(F32)
        return jnp.sum(wide * wide, axis=0, keepdims=True)

    def receive(level, h):
        chunk_copy(level, h).wait_recv()
        for p in order:
            table[h, level * n + partner(p)] = recv[level, h, p - 1]

    pl.semaphore_wait(barrier, n - 1 + m - 1)
    for p in order:
        need_copy(p).start()
    for i in range(1, levels):
        fetch(noise_hbm, noise, noise_sem, i).start()
        fetch(diag_hbm, diag, diag_sem, i).start()

    fetch(noise_hbm, noise, noise_sem, 0).wait()
    fetch(diag_hbm, diag, diag_sem, 0).wait()
    for s in range(slot_dev):
        x = jnp.dot(noise[0, s], diag[0, s], preferred_element_type=F32).astype(BF16)
        own[0, s] = x
        sums[0, pl.ds(s, 1), :] = squares(x)

    for p in order:
        need_copy(p).wait_recv()
        block = own[0, want_v[p - 1][0, 0]]
        for h in range(CHUNKS):
            send[0, h, p - 1] = block[h * part : (h + 1) * part]
        block_copy(0, 0, p).start()
    for h in range(1, CHUNKS):
        for p in order:
            block_copy(0, h, p).start()
    coup_fetch(0).start()
    coup_fetch(1).start()

    mine = need[me]
    wants = [want_v[p - 1] for p in order] + [mine]
    slots = lax.broadcasted_iota(I32, (slot_dev, 128), 0)
    first = slots + n
    for i in range(n - 2, -1, -1):
        first = jnp.where(wants[i] == slots, i, first)
    rank = jnp.zeros((slot_dev, 128), I32)
    for s in range(slot_dev):
        rank = rank + (first[s : s + 1] < first).astype(I32)
    turn = jnp.zeros((slot_dev, 128), I32)
    for s in range(slot_dev):
        turn = turn + jnp.where(rank[s : s + 1] == slots, s, 0)
    index_v[pl.ds(0, slot_dev), :] = turn
    index_v[pl.ds(slot_dev, slot_dev), :] = rank
    for i in range(n):
        index_v[pl.ds(2 * slot_dev + i, 1), :] = jnp.sum(
            jnp.where(wants[i] == slots, rank, 0), axis=0, keepdims=True
        )
    index_v[pl.ds(2 * slot_dev + n, 1), :] = mine
    copy = pltpu.make_async_copy(index_v, index, index_sem)
    copy.start()
    copy.wait()
    pat_copy.wait()

    for h in range(CHUNKS):
        table[h, me] = own[0, index[2 * slot_dev + n, 0], pl.ds(h * part, part), :]
    for level in range(1, levels):
        fetch(noise_hbm, noise, noise_sem, level).wait()
        fetch(diag_hbm, diag, diag_sem, level).wait()

    for level in range(1, levels - 1):
        coup_fetch(level - 1).wait()
        for h in range(CHUNKS):
            rows = pl.ds(h * part, part)
            receive(level - 1, h)
            done = rest(level, index[0, level], h)
            for i in range(slot_dev):
                rounded = done
                if i + 1 < slot_dev:
                    done = rest(level, index[i + 1, level], h)
                placed[level - 1, i, rows, :] = finish(level, index[i, level], rounded)
                for j in range(i, min(i + 1, n - 1) if i + 1 < slot_dev else n - 1):
                    at = index[2 * slot_dev + j, level]
                    send[level, h, order[j] - 1] = placed[level - 1, at, rows, :]
                    block_copy(level, h, order[j]).start()
            if h == CHUNKS - 1 and level + 1 < levels - 1:
                coup_fetch(level + 1).start()
            table[h, level * n + me] = placed[
                level - 1, index[2 * slot_dev + n - 1, level], rows, :
            ]
        for s in range(slot_dev):
            x = placed[level - 1, index[slot_dev + s, level]]
            own[level, s] = x
            sums[level, pl.ds(s, 1), :] = squares(x)

    last = levels - 1

    def var_copy(o, i):
        at = (pl.ds(0, last), pl.ds(last, 1))[i]
        return pltpu.make_async_remote_copy(
            src_ref=sums.at[at],
            dst_ref=vrecv.at[o - 1, at],
            send_sem=vsend_sem.at[i, o - 1],
            recv_sem=vrecv_sem.at[i, o - 1],
            device_id={"samp": lax.rem(q + o, m)},
            device_id_type=MESH,
        )

    for o in range(1, m):
        var_copy(o, 0).start()
    coup_fetch(last - 1).wait()
    for h in range(CHUNKS):
        rows = pl.ds(h * part, part)
        receive(last - 1, h)
        for s in range(slot_dev):
            x = finish(last, s, rest(last, s, h))
            own[last, s, rows, :] = x
            found = squares(x)
            if h > 0:
                found = found + sums[last, pl.ds(s, 1), :]
            sums[last, pl.ds(s, 1), :] = found
    for o in range(1, m):
        var_copy(o, 1).start()
    for level in range(levels - 1):
        for h in range(CHUNKS):
            chunk_copy(level, h).wait_send()
    for p in order:
        need_copy(p).wait_send()
    for i in range(2):
        for o in range(1, m):
            var_copy(o, i).wait()
    total = sums[...]
    for o in range(1, m):
        total = total + vrecv[o - 1]
    var_ref[...] = total * (1.0 / (samp * m))


def hand_out(x, v, y_hbm, w_hbm, sem):
    copies = [
        pltpu.make_async_copy(x, y_hbm, sem.at[0]),
        pltpu.make_async_copy(v, w_hbm, sem.at[1]),
    ]
    for copy in copies:
        copy.start()
    for copy in copies:
        copy.wait()


def body(n, m, noise, diag, coupling, pattern):
    levels, slot_dev, samp, b = noise.shape
    fan = coupling.shape[2]
    part = samp // CHUNKS
    any_spec = pl.BlockSpec(memory_space=pl.ANY)
    vmem_spec = pl.BlockSpec(memory_space=pltpu.VMEM)
    dma = pltpu.SemaphoreType.DMA
    coupling = coupling.reshape(levels - 1, slot_dev, fan * b, b)
    lines = 2 * slot_dev + -(-(n + 1) // 8) * 8
    solved = pl.pallas_call(
        functools.partial(kernel, n, m),
        out_shape=(
            jax.ShapeDtypeStruct(noise.shape, BF16),
            jax.ShapeDtypeStruct((levels, slot_dev, b), F32),
        ),
        in_specs=[any_spec] * 4,
        out_specs=(vmem_spec, vmem_spec),
        scratch_shapes=[
            pltpu.SMEM(pattern.shape, I32),
            pltpu.VMEM(pattern.shape, I32),
            pltpu.VMEM(noise.shape, BF16),
            pltpu.VMEM(diag.shape, BF16),
            pltpu.VMEM((levels - 2, slot_dev, samp, b), BF16),
            pltpu.VMEM((CHUNKS, (levels - 1) * n, part, b), BF16),
            pltpu.VMEM((levels - 1, CHUNKS, n - 1, part, b), BF16),
            pltpu.VMEM((levels - 1, CHUNKS, n - 1, part, b), BF16),
            pltpu.VMEM((n, 1, 128), I32),
            pltpu.VMEM((n - 1, 1, 128), I32),
            pltpu.VMEM((lines, 128), I32),
            pltpu.SMEM((lines, 128), I32),
            pltpu.VMEM((levels, slot_dev, b), F32),
            pltpu.VMEM((m - 1, levels, slot_dev, b), F32),
            dma((2,)),
            dma((levels,)),
            dma((levels,)),
            dma((levels - 1,)),
            dma((levels - 1, CHUNKS)),
            dma((levels - 1, CHUNKS)),
            dma((n - 1,)),
            dma((n - 1,)),
            dma,
            dma((2, m - 1)),
            dma((2, m - 1)),
        ]
        + [pltpu.VMEM(coupling.shape[1:], BF16)] * (levels - 1),
        compiler_params=pltpu.CompilerParams(
            collective_id=0, has_side_effects=True, vmem_limit_bytes=48 * 1024 * 1024
        ),
    )(*(pltpu.with_memory_space_constraint(a, pltpu.HBM) for a in (pattern, noise, diag, coupling)))
    return pl.pallas_call(
        hand_out,
        out_shape=tuple(jax.ShapeDtypeStruct(a.shape, a.dtype) for a in solved),
        in_specs=[any_spec, any_spec],
        out_specs=(any_spec, any_spec),
        scratch_shapes=[dma((2,))],
        compiler_params=pltpu.CompilerParams(vmem_limit_bytes=8 * 1024 * 1024),
    )(*solved)


def solution(mesh):
    placed = (
        P(None, "rows", "samp", None),
        P(None, "rows", None, None),
        P(None, "rows", None, None, None),
        P(None, "rows", None),
    )
    return jax.shard_map(
        functools.partial(body, mesh.shape["rows"], mesh.shape["samp"]),
        mesh=mesh,
        in_specs=placed,
        out_specs=(P(None, "rows", "samp", None), P(None, "rows", None)),
        check_vma=False,
    )
```
